32 devices in a mesh: groups: 2 (over y), strip: 4 (over z), angle: 2 (over x), depth: 2 (over core).
Axes of the slice: x: 2, y: 2, z: 4, core: 2. Of those that a mesh axis runs over, the one named last changes fastest.
Arguments:
- crystal: bfloat16 [16, 2, 512, 384], P(('groups', 'depth'), None, 'strip'), parts along dimension 0, may hold values from -4 to 4
- probe: bfloat16 [2, 256, 256], replicated, may hold values from -5 to 5
- amplitude: bfloat16 [4, 2048, 256], P('angle', ('groups', 'strip', 'depth')), parts along dimension 1, may hold values from 0.5 to 8
- shear: int32 [16, 8], P(('groups', 'angle'), 'depth'), parts along dimension 0, may hold values from 0 to 15
- scan_x: int32 [4, 4, 2], P(('groups', 'angle')), parts along dimension 0, may hold values from 0 to 112
- scan_y: int32 [4, 4, 2], P(('groups', 'angle')), parts along dimension 0, may hold values from 0 to 128
- slot_angle: int32 [4, 4, 2], P(('groups', 'angle')), parts along dimension 0, may hold values from 0 to 3
- owner_slot: int32 [4, 4, 2], P(('groups', 'angle')), parts along dimension 0, may hold values from 0 to 1, each once within a row
- counts: int32 [4, 4], P(('groups', 'angle')), parts along dimension 0, may hold values from 1 to 2
Outputs:
- gradient: float32 [16, 2, 512, 384], P(('groups', 'depth'), None, ('strip', 'angle')), parts along dimension 0
The draws below stay inside these ranges and needn't reach their ends.
There are 2 independent parts, one for each index of `groups`. The reference program is written for one: setup_inputs(seed, part) draws one part's arguments, and reference() takes and returns one part's arrays. A program takes and returns all parts, laid end to end along the dimension named above; an argument that names none is the same for every part. Nothing has to cross between parts.
Inputs may be any that keep to these rules, and one draw needn't show every extreme that they name: `owner_slot`: for each angle group and home strip, the 2 entries are a permutation of 0 to 1.
All inputs are finite; a program needn't handle non-finite values.
Results may differ from the reference program's by a relative error of at most 0.02.
Values may be sent and summed in bfloat16 or wider, within the bound.
A program may use at most 64 MiB of HBM per device.

```python
import math
import jax
import jax.numpy as jnp
from jax import lax

FRAME = 256
WX = 128
SHEAR = 16
NY = 384
NZ_DEV = 4
ANG_DEV = 4
BAND = 144
M = 2
NX = 512
NZ = 8
ANGLES = 8
ANGLE_GROUPS = 2
SLOTS = 4
N_STRIP = 4
N_ANGLE = 2
N_DEPTH = 2


def set_ends(entries, rng, low, largest):
    longest = entries.shape.index(max(entries.shape))
    spots = []
    for shift in (0, 1):
        where = [jax.random.randint(jax.random.fold_in(rng, axis), (), 0, length) for axis, length in enumerate(entries.shape)]
        where[longest] = (where[longest] + shift) % entries.shape[longest]
        spots.append(tuple(where))
    return entries.at[spots[0]].set(low).at[spots[1]].set(largest)


def block_levels(key, dims, shards, smallest, high):
    factor_of = 1.0
    for dim, parts in shards:
        steps = jax.random.uniform(jax.random.fold_in(jax.random.fold_in(key, 6), dim), (parts,), jnp.float32, smallest / len(shards), high / len(shards))
        factor_of = factor_of * jnp.repeat(jnp.exp(steps), dims[dim] // parts).reshape((-1,) + (1,) * (len(dims) - 1 - dim))
    return factor_of


def centred(rng, extent, spread, bound, split=(), held_as=jnp.bfloat16):
    array = spread * jax.random.normal(rng, extent, jnp.float32)
    if split:
        array = array * block_levels(rng, extent, split, -0.22, 0.18)
    return jnp.clip(array, -bound, bound).astype(held_as)


def setup_inputs(seed: int = 0, part: int = 0) -> dict:
    key_of = jax.random.split(jax.random.key(seed), 10)
    part_keys = jax.random.split(jax.random.fold_in(key_of[9], part), 10)
    return {
        "crystal": centred(part_keys[0], (NZ, 2, NX, NY), 0.5, 4.0, ((0, 2), (2, 4))),
        "probe": centred(key_of[1], (2, FRAME, FRAME), 1.0, 5.0),
        "amplitude": jnp.clip(jnp.exp(math.log(8.0) - 2.7725887 * jax.random.uniform(part_keys[2], (SLOTS, N_STRIP * FRAME, FRAME), jnp.float32) ** block_levels(part_keys[2], (SLOTS, N_STRIP * FRAME, FRAME), ((0, 2), (1, 8)), -0.2, 0.2)), 0.5, 8.0).astype(jnp.bfloat16),
        "shear": set_ends(jax.random.randint(part_keys[3], (ANGLES, NZ), 0, SHEAR), jax.random.fold_in(part_keys[3], 1), 0, SHEAR - 1).astype(jnp.int32),
        "scan_x": set_ends(jax.random.randint(part_keys[4], (ANGLE_GROUPS, N_STRIP, M), 0, min(WX, 3 * WX - FRAME - SHEAR + 1)), jax.random.fold_in(part_keys[4], 1), 0, (min(WX, 3 * WX - FRAME - SHEAR + 1)) - 1).astype(jnp.int32),
        "scan_y": set_ends(jax.random.randint(part_keys[5], (ANGLE_GROUPS, N_STRIP, M), 0, NY - FRAME + 1), jax.random.fold_in(part_keys[5], 1), 0, NY - FRAME).astype(jnp.int32),
        "slot_angle": set_ends(jax.random.randint(part_keys[6], (ANGLE_GROUPS, N_STRIP, M), 0, ANG_DEV), jax.random.fold_in(part_keys[6], 1), 0, ANG_DEV - 1).astype(jnp.int32),
        "owner_slot": jax.vmap(lambda own: jax.random.permutation(own, M))(jax.random.split(part_keys[7], ANGLE_GROUPS * N_STRIP)).reshape((ANGLE_GROUPS, N_STRIP, M)).astype(jnp.int32),
        "counts": set_ends(jax.random.randint(part_keys[8], (ANGLE_GROUPS, N_STRIP), M // 2, M + 1), jax.random.fold_in(part_keys[8], 1), M // 2, M).astype(jnp.int32),
    }


def spot(*values):
    return tuple((jnp.asarray(value, jnp.int32) for value in values))

def dft_parts():
    index_row = jnp.arange(FRAME, dtype=jnp.int32)
    wound = index_row[:, None] * index_row[None, :] % FRAME
    phase = wound.astype(jnp.float32) * (2.0 * math.pi / FRAME)
    scaling = 1.0 / math.sqrt(FRAME)
    return ((jnp.cos(phase) * scaling).astype(jnp.bfloat16), (-jnp.sin(phase) * scaling).astype(jnp.bfloat16))

def stamp(value):
    return lax.optimization_barrier(value.astype(jnp.bfloat16)).astype(jnp.float32)

def complex_times(left, right, sign):
    out_re = left[0] * right[0] - sign * left[1] * right[1]
    out_im = left[0] * right[1] + sign * left[1] * right[0]
    return jnp.stack([out_re, out_im], axis=0)

def right_product(block, table_re, table_im, sign):
    part_re = block[0]
    part_im = block[1]
    first = jnp.dot(part_re, table_re, preferred_element_type=jnp.float32)
    second = jnp.dot(part_im, table_im, preferred_element_type=jnp.float32)
    third = jnp.dot(part_re, table_im, preferred_element_type=jnp.float32)
    fourth = jnp.dot(part_im, table_re, preferred_element_type=jnp.float32)
    return jnp.stack([first - sign * second, sign * third + fourth], axis=0)

def row_product(rows_re, rows_im, block, sign):
    part_re = block[0]
    part_im = block[1]
    first = jnp.dot(rows_re, part_re, preferred_element_type=jnp.float32)
    second = jnp.dot(rows_im, part_im, preferred_element_type=jnp.float32)
    third = jnp.dot(rows_im, part_re, preferred_element_type=jnp.float32)
    fourth = jnp.dot(rows_re, part_im, preferred_element_type=jnp.float32)
    return jnp.stack([first - sign * second, sign * third + fourth], axis=0)

def reference(crystal, probe, amplitude, shear, scan_x, scan_y, slot_angle, owner_slot, counts):
    table_re, table_im = dft_parts()
    pad_re = jnp.pad(table_re, ((BAND, BAND), (0, 0)))
    pad_im = jnp.pad(table_im, ((BAND, BAND), (0, 0)))
    probe_pad = jnp.pad(probe, ((0, 0), (BAND, BAND), (0, 0)))
    crystal_pad = jnp.pad(crystal, ((0, 0), (0, 0), (SHEAR, SHEAR), (0, 0)))
    depth_rows = FRAME // N_DEPTH
    quarter = N_STRIP // 4
    band_index = jnp.arange(BAND, dtype=jnp.int32)

    def group_step(summed, group):
        shear_rows = lax.dynamic_slice_in_dim(shear, jnp.asarray(group * ANG_DEV, jnp.int32), ANG_DEV, 0)
        offsets = scan_x[group]
        columns = scan_y[group]
        angles = slot_angle[group]
        owners = owner_slot[group]
        limits = counts[group]

        def pattern_step(gradient_pad, item):
            home = item // M
            slot_id = item % M
            living = (slot_id < limits[home]).astype(jnp.float32)
            offset = offsets[home, slot_id]
            column = columns[home, slot_id]
            quota = owners[home, slot_id]
            owner = (home + 4 * (quota % quarter) + 1) % N_STRIP
            shifts = shear_rows[angles[home, slot_id]]
            starts = [jnp.asarray(band_k * WX - offset - SHEAR + BAND, jnp.int32) for band_k in range(3)]
            rows_re = [lax.dynamic_slice_in_dim(pad_re, first_row, BAND, 0) for first_row in starts]
            rows_im = [lax.dynamic_slice_in_dim(pad_im, first_row, BAND, 0) for first_row in starts]
            probes = [lax.dynamic_slice_in_dim(probe_pad, first_row, BAND, 1).astype(jnp.float32) for first_row in starts]
            spectrum = jnp.zeros((2, FRAME, FRAME), jnp.float32)
            for slab in range(N_DEPTH):
                slab_sum = jnp.zeros((2, FRAME, FRAME), jnp.float32)
                for band_k in range(3):
                    accum = jnp.zeros((2, BAND, FRAME), jnp.float32)
                    for layer_index in range(slab * NZ_DEV, (slab + 1) * NZ_DEV):
                        lift = shifts[layer_index]
                        window = lax.dynamic_slice(crystal_pad[layer_index], spot(0, (home + band_k) * WX + lift, column), (2, BAND, FRAME)).astype(jnp.float32)
                        local_row = band_index + lift - SHEAR
                        inside = ((local_row >= 0) & (local_row < WX)).astype(jnp.float32)
                        accum = accum + window * inside[None, :, None]
                    band = accum.astype(jnp.bfloat16)
                    exit_band = complex_times(probes[band_k], band.astype(jnp.float32), 1.0).astype(jnp.bfloat16)
                    section = right_product(exit_band, table_re, table_im, 1.0).astype(jnp.bfloat16)
                    slab_sum = slab_sum + row_product(rows_re[band_k].T, rows_im[band_k].T, section, 1.0)
                spectrum = spectrum + stamp(slab_sum)
            measured = lax.dynamic_slice(amplitude, spot(group * M + quota, owner * FRAME, 0), (1, FRAME, FRAME))[0].astype(jnp.float32)
            magnitude = jnp.sqrt(spectrum[0] * spectrum[0] + spectrum[1] * spectrum[1])
            factor = (1.0 - measured / jnp.maximum(magnitude, 1.0)) * living
            residual = (spectrum * factor[None]).astype(jnp.bfloat16)
            inverse_rows = right_product(residual, table_re, table_im, -1.0).astype(jnp.bfloat16)
            for band_k in range(3):
                back_total = jnp.zeros((2, BAND, FRAME), jnp.float32)
                for block_index in range(N_DEPTH):
                    row_low = block_index * depth_rows
                    wave = row_product(rows_re[band_k][:, row_low:row_low + depth_rows], rows_im[band_k][:, row_low:row_low + depth_rows], inverse_rows[:, row_low:row_low + depth_rows], -1.0)
                    back_total = back_total + stamp(complex_times(probes[band_k], wave, -1.0))
                back_band = stamp(back_total)
                for layer_index in range(NZ):
                    lift = shifts[layer_index]
                    local_row = band_index + lift - SHEAR
                    inside = ((local_row >= 0) & (local_row < WX)).astype(jnp.float32)
                    position = spot(layer_index, 0, (home + band_k) * WX + lift, column)
                    current = lax.dynamic_slice(gradient_pad, position, (1, 2, BAND, FRAME))
                    gradient_pad = lax.dynamic_update_slice(gradient_pad, current + (back_band * inside[None, :, None])[None], position)
            return (gradient_pad, None)
        items = jnp.arange((N_STRIP - 2) * M, dtype=jnp.int32)
        start_pad = jnp.zeros((NZ, 2, NX + 2 * SHEAR, NY), jnp.float32)
        gradient_pad, unused = lax.scan(pattern_step, start_pad, items)
        cropped = gradient_pad[:, :, SHEAR:SHEAR + NX]
        return (summed + stamp(cropped), None)
    summed, unused = lax.scan(group_step, jnp.zeros((NZ, 2, NX, NY), jnp.float32), jnp.arange(N_ANGLE, dtype=jnp.int32))
    return summed * (1.0 / ANGLES)
```

```python
import functools

import jax
import jax.numpy as jnp
import numpy as np
from jax import lax
from jax.experimental import pallas as pl
from jax.experimental.pallas import tpu as pltpu
from jax.sharding import PartitionSpec as P

FRAME = 256
WX = 128
REACHES = 3
ROWS = (WX, FRAME, FRAME - WX)
BASES = (0, 0, WX)
MESH = pl.DeviceIdType.MESH


def dft_tables():
    index_row = np.arange(FRAME)
    phase = (index_row[:, None] * index_row[None, :] % FRAME) * (2.0 * np.pi / FRAME)
    real = np.cos(phase) / np.sqrt(FRAME)
    imag = -np.sin(phase) / np.sqrt(FRAME)
    table = np.block([[real, imag], [-imag, real]]).astype(np.float32)
    return jnp.asarray(table, jnp.bfloat16), jnp.asarray(table.T, jnp.bfloat16)


def dot(left, right):
    return jnp.dot(left, right, preferred_element_type=jnp.float32)


def differences(rows, columns):
    shape = (rows, columns)
    return lax.broadcasted_iota(jnp.int32, shape, 1) - lax.broadcasted_iota(jnp.int32, shape, 0)


def one_hot(mask):
    return jnp.where(mask, 1.0, 0.0).astype(jnp.bfloat16)


def kernel(
    sizes,
    crystal,
    probe,
    amplitude,
    table,
    table_t,
    shear,
    scan_x,
    scan_y,
    slot_angle,
    owner_slot,
    counts,
    out,
    film,
    sent0,
    sent1,
    sent2,
    got0,
    got1,
    got2,
    measured,
    back,
    home0,
    home1,
    home2,
    placed,
    total,
    grad_out,
    grad_in,
    film_send,
    film_recv,
    amp_send,
    amp_recv,
    back_send,
    back_recv,
    grad_send,
    grad_recv,
):
    strips, angle_devs, depths, layers, slots, columns = sizes
    quarter = strips // 4
    half = slots // depths
    share = WX // angle_devs
    sent = (sent0, sent1, sent2)
    got = (got0, got1, got2)
    homes = (home0, home1, home2)
    s = lax.axis_index("strip")
    a = lax.axis_index("angle")
    d = lax.axis_index("depth")

    def rcopy(source, target, send_sem, recv_sem, **where):
        return pltpu.make_async_remote_copy(
            source, target, send_sem, recv_sem, device_id=where, device_id_type=MESH
        )

    def wrap(strip):
        return lax.rem(strip + 4 * strips, strips)

    barrier = pltpu.get_barrier_semaphore()
    shifts = set()
    for k in range(REACHES):
        for t in range(quarter):
            shifts |= {(1 - k + 4 * t) % strips, (k - 1 - 4 * t) % strips}
    expected = jnp.int32(angle_devs - 1 + depths - 1)
    for step in range(1, angle_devs):
        pl.semaphore_signal(
            barrier, 1, device_id={"angle": lax.rem(a + step, angle_devs)}, device_id_type=MESH
        )
    for step in range(1, depths):
        pl.semaphore_signal(
            barrier, 1, device_id={"depth": lax.rem(d + step, depths)}, device_id_type=MESH
        )
    for shift in sorted(shifts - {0}):
        peer = wrap(s + shift)
        if quarter == 1:
            close = jnp.abs(peer - s) == 1
        else:
            close = peer >= 0
        expected = expected + jnp.where(close, depths, 0)

        @pl.when(close)
        def _():
            for other in range(depths):
                pl.semaphore_signal(
                    barrier, 1, device_id={"strip": peer, "depth": other}, device_id_type=MESH
                )

    for layer in range(layers):
        for part in range(2):
            film[layer * WX : (layer + 1) * WX, part * columns : (part + 1) * columns] = crystal[
                layer, part
            ]
    pl.semaphore_wait(barrier, expected)

    def pick(ref, home, quota):
        value = jnp.int32(0)
        for m in range(slots):
            value = value + jnp.where(owner_slot[0, home, m] == quota, ref[0, home, m], 0)
        return value

    for other in range(depths):
        block = amplitude.at[other * half : (other + 1) * half]

        @pl.when(d != other)
        def _():
            rcopy(block, measured.at[d], amp_send.at[other], amp_recv.at[d], depth=other).start()

        @pl.when(d == other)
        def _():
            measured[d] = amplitude[other * half : (other + 1) * half]

    def film_copy(k, q):
        owner = wrap(s - k + 4 * (q % quarter) + 1)
        return rcopy(
            sent[k].at[q],
            got[k].at[d, q % half],
            film_send.at[k, q],
            film_recv.at[k, d, q % half],
            strip=owner,
            depth=q // half,
        )

    def own_strip(k, q):
        return (1 - k + 4 * (q % quarter)) % strips == 0

    for k in (0, 2, 1):
        home = s - k
        rows = ROWS[k]

        @pl.when((home >= 0) & (home <= strips - 3))
        def _():
            for q in range(slots):
                offset = pick(scan_x, home, q) - WX * k + BASES[k]
                angle = pick(slot_angle, home, q)
                corner = pick(scan_y, home, q)
                gap = differences(rows, WX)
                picks = jnp.concatenate(
                    [one_hot(gap == offset + shear[angle, z]) for z in range(layers)], axis=1
                )
                tall = dot(picks, film[...]).astype(jnp.bfloat16)
                window = one_hot(differences(FRAME, columns) == corner).T
                wave = jnp.concatenate(
                    [dot(tall[:, :columns], window), dot(tall[:, columns:], window)], axis=1
                ).astype(jnp.bfloat16)
                if own_strip(k, q):

                    @pl.when(d == q // half)
                    def _():
                        got[k][d, q % half] = wave

                    @pl.when(d != q // half)
                    def _():
                        sent[k][q] = wave
                        film_copy(k, q).start()
                else:
                    sent[k][q] = wave
                    film_copy(k, q).start()

    for other in range(depths):

        @pl.when(d != other)
        def _():
            rcopy(
                amplitude.at[other * half : (other + 1) * half],
                measured.at[other],
                amp_send.at[other],
                amp_recv.at[other],
                depth=other,
            ).wait_recv()

    for lane in range(half):
        quota = d * half + lane
        home = wrap(s - 1 - 4 * lax.rem(quota, quarter))

        @pl.when(home <= strips - 3)
        def _():
            for k in (1, 0, 2):
                for source in range(depths):
                    local = (wrap(home + k) == s) & (d == source)

                    @pl.when(jnp.logical_not(local))
                    def _():
                        rcopy(
                            sent[k].at[lane],
                            got[k].at[source, lane],
                            film_send.at[k, lane],
                            film_recv.at[k, source, lane],
                            strip=wrap(home + k),
                            depth=source,
                        ).wait_recv()

            def gathered(ref, low, high):
                value = ref[0, lane, low:high].astype(jnp.float32)
                for source in range(1, depths):
                    value = value + ref[source, lane, low:high].astype(jnp.float32)
                return value

            whole = jnp.concatenate(
                [
                    gathered(got1, 0, WX) + gathered(got0, 0, WX),
                    gathered(got1, WX, FRAME) + gathered(got2, 0, FRAME - WX),
                ],
                axis=0,
            )
            probe_re = probe[0].astype(jnp.float32)
            probe_im = probe[1].astype(jnp.float32)
            film_re, film_im = whole[:, :FRAME], whole[:, FRAME:]
            exit_wave = jnp.concatenate(
                [probe_re * film_re - probe_im * film_im, probe_re * film_im + probe_im * film_re],
                axis=1,
            ).astype(jnp.bfloat16)
            section = dot(exit_wave, table[...]).astype(jnp.bfloat16)
            spectrum = dot(
                table_t[...], jnp.concatenate([section[:, :FRAME], section[:, FRAME:]], axis=0)
            )
            spec_re, spec_im = spectrum[:FRAME], spectrum[FRAME:]
            magnitude = jnp.sqrt(spec_re * spec_re + spec_im * spec_im)
            levels = jnp.concatenate(
                [measured[source, lane] for source in range(depths)], axis=0
            ).astype(jnp.float32)
            slot = jnp.int32(0)
            for m in range(slots):
                slot = slot + jnp.where(owner_slot[0, home, m] == quota, m, 0)
            live = jnp.where(slot < counts[0, home], 1.0, 0.0).astype(jnp.float32)
            factor = (1.0 - levels / jnp.maximum(magnitude, 1.0)) * live
            residual = jnp.concatenate([spec_re * factor, spec_im * factor], axis=1).astype(
                jnp.bfloat16
            )
            inverse = dot(residual, table_t[...]).astype(jnp.bfloat16)
            wave = dot(
                table[...], jnp.concatenate([inverse[:, :FRAME], inverse[:, FRAME:]], axis=0)
            )
            wave_re, wave_im = wave[:FRAME], wave[FRAME:]
            back[lane] = jnp.concatenate(
                [probe_re * wave_re + probe_im * wave_im, probe_re * wave_im - probe_im * wave_re],
                axis=1,
            ).astype(jnp.bfloat16)

    def back_copy(k, q, home, other):
        return rcopy(
            back.at[q % half, BASES[k] : BASES[k] + ROWS[k]],
            homes[k].at[q],
            back_send.at[k, q % half, other],
            back_recv.at[k, q],
            strip=wrap(home + k),
            depth=other,
        )

    def returns(act, keep):
        for q in range(slots):
            home = wrap(s - 1 - 4 * (q % quarter))

            @pl.when((home <= strips - 3) & (d == q // half))
            def _():
                for k in (0, 2, 1):
                    for other in range(depths):
                        if own_strip(k, q) and other == q // half:
                            if keep:
                                homes[k][q] = back[q % half, BASES[k] : BASES[k] + ROWS[k]]
                        else:
                            act(back_copy(k, q, home, other))

    returns(lambda copy: copy.start(), True)

    for k in range(REACHES):
        home = s - k
        rows = ROWS[k]
        base = sum(ROWS[:k]) * slots

        @pl.when((home >= 0) & (home <= strips - 3))
        def _():
            for q in range(slots):
                if own_strip(k, q):

                    @pl.when(d != q // half)
                    def _():
                        back_copy(k, q, home, q // half).wait_recv()
                else:
                    back_copy(k, q, home, q // half).wait_recv()
                corner = pick(scan_y, home, q)
                window = one_hot(differences(FRAME, columns) == corner)
                value = homes[k][q]
                placed[base + q * rows : base + (q + 1) * rows, :columns] = dot(
                    value[:, :FRAME], window
                ).astype(jnp.bfloat16)
                placed[base + q * rows : base + (q + 1) * rows, columns:] = dot(
                    value[:, FRAME:], window
                ).astype(jnp.bfloat16)

    def grad_copy(step, z):
        other = lax.rem(a + step, angle_devs)
        return rcopy(
            grad_out.at[other, z],
            grad_in.at[step, z],
            grad_send.at[step, z],
            grad_recv.at[step, z],
            angle=other,
        )

    for z in range(layers):
        total[...] = jnp.zeros_like(total)
        for k in range(REACHES):
            home = s - k
            rows = ROWS[k]
            base = sum(ROWS[:k]) * slots

            @pl.when((home >= 0) & (home <= strips - 3))
            def _():
                picks = []
                for q in range(slots):
                    offset = pick(scan_x, home, q) - WX * k + BASES[k]
                    lift = shear[pick(slot_angle, home, q), z]
                    picks.append(one_hot(differences(WX, rows) == -(offset + lift)))
                total[...] += dot(
                    jnp.concatenate(picks, axis=1), placed[base : base + slots * rows]
                )

        for other in range(angle_devs):
            grad_out[other, z] = total[other * share : (other + 1) * share].astype(jnp.bfloat16)
        for step in range(1, angle_devs):
            grad_copy(step, z).start()

    scaling = 1.0 / (shear.shape[0] * angle_devs)
    for z in range(layers):
        value = grad_out[a, z].astype(jnp.float32)
        for step in range(1, angle_devs):
            grad_copy(step, z).wait_recv()
            value = value + grad_in[step, z].astype(jnp.float32)
        value = value * scaling
        for part in range(2):
            out[z, part] = value[:, part * columns : (part + 1) * columns]

    for other in range(depths):

        @pl.when(d != other)
        def _():
            rcopy(
                amplitude.at[other * half : (other + 1) * half],
                measured.at[d],
                amp_send.at[other],
                amp_recv.at[d],
                depth=other,
            ).wait_send()

    for k in range(REACHES):
        home = s - k

        @pl.when((home >= 0) & (home <= strips - 3))
        def _():
            for q in range(slots):
                if own_strip(k, q):

                    @pl.when(d != q // half)
                    def _():
                        film_copy(k, q).wait_send()
                else:
                    film_copy(k, q).wait_send()

    returns(lambda copy: copy.wait_send(), False)
    for z in range(layers):
        for step in range(1, angle_devs):
            grad_copy(step, z).wait_send()


def body(sizes_of, crystal, probe, amplitude, shear, scan_x, scan_y, slot_angle, owner_slot, counts):
    strips, angle_devs, depths = sizes_of
    layers, _, _, columns = crystal.shape
    slots = owner_slot.shape[2]
    half = slots // depths
    share = WX // angle_devs
    table, table_t = dft_tables()
    bf16 = jnp.bfloat16
    vmem = pl.BlockSpec(memory_space=pltpu.VMEM)
    smem = pl.BlockSpec(memory_space=pltpu.SMEM)
    dma = pltpu.SemaphoreType.DMA
    scratch = [pltpu.VMEM((layers * WX, 2 * columns), bf16)]
    scratch += [pltpu.VMEM((slots, rows, 2 * FRAME), bf16) for rows in ROWS]
    scratch += [pltpu.VMEM((depths, half, rows, 2 * FRAME), bf16) for rows in ROWS]
    scratch += [
        pltpu.VMEM((depths, half, FRAME // depths, FRAME), bf16),
        pltpu.VMEM((half, FRAME, 2 * FRAME), bf16),
    ]
    scratch += [pltpu.VMEM((slots, rows, 2 * FRAME), bf16) for rows in ROWS]
    scratch += [
        pltpu.VMEM((sum(ROWS) * slots, 2 * columns), bf16),
        pltpu.VMEM((WX, 2 * columns), jnp.float32),
        pltpu.VMEM((angle_devs, layers, share, 2 * columns), bf16),
        pltpu.VMEM((angle_devs, layers, share, 2 * columns), bf16),
        dma((REACHES, slots)),
        dma((REACHES, depths, half)),
        dma((depths,)),
        dma((depths,)),
        dma((REACHES, half, depths)),
        dma((REACHES, slots)),
        dma((angle_devs, layers)),
        dma((angle_devs, layers)),
    ]
    return pl.pallas_call(
        functools.partial(kernel, (strips, angle_devs, depths, layers, slots, columns)),
        out_shape=jax.ShapeDtypeStruct((layers, 2, share, columns), jnp.float32),
        in_specs=[vmem] * 5 + [smem] * 6,
        out_specs=vmem,
        scratch_shapes=scratch,
        compiler_params=pltpu.CompilerParams(collective_id=0, has_side_effects=True),
    )(
        crystal,
        probe,
        amplitude,
        table,
        table_t,
        shear,
        scan_x,
        scan_y,
        slot_angle,
        owner_slot,
        counts,
    )


def solution(mesh):
    placed = (
        P(("groups", "depth"), None, "strip", None),
        P(),
        P("angle", ("groups", "strip", "depth"), None),
        P(("groups", "angle"), "depth"),
        P(("groups", "angle"), None, None),
        P(("groups", "angle"), None, None),
        P(("groups", "angle"), None, None),
        P(("groups", "angle"), None, None),
        P(("groups", "angle"), None),
    )
    sizes_of = (mesh.shape["strip"], mesh.shape["angle"], mesh.shape["depth"])
    return jax.shard_map(
        functools.partial(body, sizes_of),
        mesh=mesh,
        in_specs=placed,
        out_specs=P(("groups", "depth"), None, ("strip", "angle"), None),
        check_vma=False,
    )
```

```python
import functools

import jax
import jax.numpy as jnp
import numpy as np
from jax import lax
from jax.experimental import pallas as pl
from jax.experimental.pallas import tpu as pltpu
from jax.sharding import PartitionSpec as P

FRAME = 256
WX = 128
SHEAR = 16
REACHES = 3
ROWS = (WX, FRAME, FRAME - WX)
BASES = (0, 0, WX)
MESH = pl.DeviceIdType.MESH


def dft_tables():
    index_row = np.arange(FRAME)
    phase = (index_row[:, None] * index_row[None, :] % FRAME) * (2.0 * np.pi / FRAME)
    real = np.cos(phase) / np.sqrt(FRAME)
    imag = -np.sin(phase) / np.sqrt(FRAME)
    table = np.block([[real, imag], [-imag, real]]).astype(np.float32)
    return jnp.asarray(table, jnp.bfloat16), jnp.asarray(table.T, jnp.bfloat16)


def dot(left, right):
    return jnp.dot(left, right, preferred_element_type=jnp.float32)


def differences(rows, columns):
    shape = (rows, columns)
    return lax.broadcasted_iota(jnp.int32, shape, 1) - lax.broadcasted_iota(jnp.int32, shape, 0)


def one_hot(mask):
    return jnp.where(mask, 1.0, 0.0).astype(jnp.bfloat16)


class Meta:
    def __init__(self, lifts, owner_slot, slots, lead):
        self.lifts, self.owner_slot = lifts, owner_slot
        self.slots, self.lead = slots, lead

    def shear(self, angle, z):
        return self.lifts[self.lead + (angle, z)]

    def pick(self, ref, home, quota):
        value = jnp.int32(0)
        for m in range(self.slots):
            at = self.lead + (0, m, home)
            value = value + jnp.where(self.owner_slot[at] == quota, ref[at], 0)
        return value

    def slot(self, home, quota):
        value = jnp.int32(0)
        for m in range(self.slots):
            at = self.lead + (0, m, home)
            value = value + jnp.where(self.owner_slot[at] == quota, m, 0)
        return value


def kernel(
    sizes,
    crystal,
    probe_in,
    amplitude,
    table_in,
    table_t_in,
    shear,
    scan_x,
    scan_y,
    slot_angle,
    owner_slot,
    counts,
    shear_in,
    scan_y_in,
    slot_angle_in,
    owner_slot_in,
    windows,
    shear_out,
    scan_y_out,
    slot_angle_out,
    owner_slot_out,
    film,
    probe,
    table,
    table_t,
    sent0,
    sent1,
    sent2,
    got0,
    got1,
    got2,
    measured,
    cuts,
    load_sem,
    film_send,
    film_recv,
    amp_send,
    amp_recv,
    meta_send,
    meta_recv,
    cut_send,
    pass_send,
    win_recv,
):
    strips, angle_devs, depths, layers, slots, columns = sizes
    quarter = strips // 4
    half = slots // depths
    share = WX // angle_devs
    reach = share + SHEAR
    sent = (sent0, sent1, sent2)
    got = (got0, got1, got2)
    s = lax.axis_index("strip")
    a = lax.axis_index("angle")
    d = lax.axis_index("depth")
    meta = Meta(shear, owner_slot, slots, ())

    def rcopy(source, target, send_sem, recv_sem, **where):
        return pltpu.make_async_remote_copy(
            source, target, send_sem, recv_sem, device_id=where, device_id_type=MESH
        )

    def wrap(strip):
        return lax.rem(strip + 4 * strips, strips)

    loads = [
        pltpu.make_async_copy(
            crystal.at[layer, part],
            film.at[layer * WX : (layer + 1) * WX, part * columns : (part + 1) * columns],
            load_sem.at[layer * 2 + part],
        )
        for layer in range(layers)
        for part in range(2)
    ]
    late = [
        pltpu.make_async_copy(source, target, load_sem.at[2 * layers + i])
        for i, (source, target) in enumerate(
            ((probe_in, probe), (table_in, table), (table_t_in, table_t))
        )
    ]
    for copy in loads + late:
        copy.start()

    barrier = pltpu.get_barrier_semaphore()
    shifts = set()
    for k in range(REACHES):
        for t in range(quarter):
            shifts |= {(1 - k + 4 * t) % strips, (k - 1 - 4 * t) % strips}
    expected = jnp.int32(0)
    for shift in sorted(shifts | {0}):
        peer = wrap(s + shift)
        if quarter == 1 and shift:
            close = jnp.abs(peer - s) == 1
        else:
            close = peer >= 0
        near = angle_devs + depths - 1 - (1 if shift == 0 else 0)
        expected = expected + jnp.where(close, near, 0)

        @pl.when(close)
        def _():
            for step in range(angle_devs):
                if shift or step:
                    place = {"strip": peer, "angle": lax.rem(a + step, angle_devs)}
                    pl.semaphore_signal(barrier, 1, device_id=place, device_id_type=MESH)
            for step in range(1, depths):
                place = {"strip": peer, "depth": lax.rem(d + step, depths)}
                pl.semaphore_signal(barrier, 1, device_id=place, device_id_type=MESH)

    for copy in loads:
        copy.wait()

    def film_copy(k, q):
        owner = wrap(s - k + 4 * (q % quarter) + 1)
        return rcopy(
            sent[k].at[q],
            got[k].at[d, q % half],
            film_send.at[k, q],
            film_recv.at[k, d, q % half],
            strip=owner,
            depth=q // half,
        )

    def own_strip(k, q):
        return (1 - k + 4 * (q % quarter)) % strips == 0

    def project(k, q):
        home = s - k
        offset = meta.pick(scan_x, home, q) - WX * k + BASES[k]
        angle = meta.pick(slot_angle, home, q)
        corner = meta.pick(scan_y, home, q)
        gap = differences(ROWS[k], WX)
        picks = jnp.concatenate(
            [one_hot(gap == offset + meta.shear(angle, z)) for z in range(layers)], axis=1
        )
        tall = dot(picks, film[...]).astype(jnp.bfloat16)
        window = one_hot(differences(columns, FRAME) == -corner)
        return jnp.concatenate(
            [dot(tall[:, :columns], window), dot(tall[:, columns:], window)], axis=1
        ).astype(jnp.bfloat16)

    def reached(k):
        return (s - k >= 0) & (s - k <= strips - 3)

    for k in (0, 2):

        @pl.when(reached(k))
        def _():
            for q in range(slots):
                sent[k][q] = project(k, q)

    pl.semaphore_wait(barrier, expected)

    for k in (0, 2):

        @pl.when(reached(k))
        def _():
            for q in range(slots):
                if own_strip(k, q):

                    @pl.when(d == q // half)
                    def _():
                        got[k][d, q % half] = sent[k][q]

                    @pl.when(d != q // half)
                    def _():
                        film_copy(k, q).start()
                else:
                    film_copy(k, q).start()

    def amp_copy(other):
        return rcopy(
            amplitude.at[other * half : (other + 1) * half],
            measured.at[d],
            amp_send.at[other],
            amp_recv.at[d],
            depth=other,
        )

    def amp_own(other):
        return pltpu.make_async_copy(
            amplitude.at[other * half : (other + 1) * half], measured.at[d], amp_recv.at[d]
        )

    tables = (
        (shear_in, shear_out),
        (scan_y_in, scan_y_out),
        (slot_angle_in, slot_angle_out),
        (owner_slot_in, owner_slot_out),
    )

    def meta_copies(step):
        return [
            rcopy(
                source,
                target.at[step],
                meta_send.at[step, i],
                meta_recv.at[step, i],
                angle=lax.rem(a + step, angle_devs),
            )
            for i, (source, target) in enumerate(tables)
        ]

    for other in range(depths):

        @pl.when(d != other)
        def _():
            amp_copy(other).start()

        @pl.when(d == other)
        def _():
            amp_own(other).start()

    for step in range(1, angle_devs):
        for copy in meta_copies(step):
            copy.start()

    @pl.when(reached(1))
    def _():
        for q in range(slots):
            if own_strip(1, q):

                @pl.when(d == q // half)
                def _():
                    got[1][d, q % half] = project(1, q)

                @pl.when(d != q // half)
                def _():
                    sent[1][q] = project(1, q)
                    film_copy(1, q).start()
            else:
                sent[1][q] = project(1, q)
                film_copy(1, q).start()

    for copy in late:
        copy.wait()
    for other in range(depths):

        @pl.when(d != other)
        def _():
            rcopy(
                amplitude.at[other * half : (other + 1) * half],
                measured.at[other],
                amp_send.at[other],
                amp_recv.at[other],
                depth=other,
            ).wait_recv()

        @pl.when(d == other)
        def _():
            amp_own(other).wait()

    for lane in range(half):
        quota = d * half + lane
        home = wrap(s - 1 - 4 * lax.rem(quota, quarter))

        @pl.when(home <= strips - 3)
        def _():
            for k in (1, 0, 2):
                for source in range(depths):
                    local = (wrap(home + k) == s) & (d == source)

                    @pl.when(jnp.logical_not(local))
                    def _():
                        rcopy(
                            sent[k].at[lane],
                            got[k].at[source, lane],
                            film_send.at[k, lane],
                            film_recv.at[k, source, lane],
                            strip=wrap(home + k),
                            depth=source,
                        ).wait_recv()

            def gathered(ref, low, high):
                value = ref[0, lane, low:high].astype(jnp.float32)
                for source in range(1, depths):
                    value = value + ref[source, lane, low:high].astype(jnp.float32)
                return value

            whole = jnp.concatenate(
                [
                    gathered(got1, 0, WX) + gathered(got0, 0, WX),
                    gathered(got1, WX, FRAME) + gathered(got2, 0, FRAME - WX),
                ],
                axis=0,
            )
            probe_re = probe[0].astype(jnp.float32)
            probe_im = probe[1].astype(jnp.float32)
            film_re, film_im = whole[:, :FRAME], whole[:, FRAME:]
            exit_wave = jnp.concatenate(
                [probe_re * film_re - probe_im * film_im, probe_re * film_im + probe_im * film_re],
                axis=1,
            ).astype(jnp.bfloat16)
            section = dot(exit_wave, table[...]).astype(jnp.bfloat16)
            spectrum = dot(
                table_t[...], jnp.concatenate([section[:, :FRAME], section[:, FRAME:]], axis=0)
            )
            spec_re, spec_im = spectrum[:FRAME], spectrum[FRAME:]
            magnitude = jnp.sqrt(spec_re * spec_re + spec_im * spec_im)
            levels = jnp.concatenate(
                [measured[source, lane] for source in range(depths)], axis=0
            ).astype(jnp.float32)
            live = meta.slot(home, quota) < counts[0, home]
            live = jnp.where(live, 1.0, 0.0).astype(jnp.float32)
            factor = (1.0 - levels / jnp.maximum(magnitude, 1.0)) * live
            residual = jnp.concatenate([spec_re * factor, spec_im * factor], axis=1).astype(
                jnp.bfloat16
            )
            inverse = dot(residual, table_t[...]).astype(jnp.bfloat16)
            wave = dot(
                table[...], jnp.concatenate([inverse[:, :FRAME], inverse[:, FRAME:]], axis=0)
            )
            wave_re, wave_im = wave[:FRAME], wave[FRAME:]
            back = jnp.concatenate(
                [probe_re * wave_re + probe_im * wave_im, probe_re * wave_im - probe_im * wave_re],
                axis=1,
            ).astype(jnp.bfloat16)
            offset = meta.pick(scan_x, home, quota)
            gap = differences(reach, FRAME)
            for k in (2, 0, 1):
                for part in range(angle_devs):
                    first = WX * k - offset + part * share - (SHEAR - 1)
                    cuts[lane, k, part] = dot(one_hot(gap == first), back).astype(jnp.bfloat16)

    def cut_copy(k, q, home, step):
        target = lax.rem(a + step, angle_devs)
        return rcopy(
            cuts.at[q % half, k, target],
            windows.at[step, k, q],
            cut_send.at[k, q % half, step],
            win_recv.at[step, k, q],
            strip=wrap(home + k),
            angle=target,
        )

    def cut_local(k, q):
        return pltpu.make_async_copy(
            cuts.at[q % half, k, a], windows.at[0, k, q], win_recv.at[0, k, q]
        )

    def pass_copy(step, k, q, other):
        return rcopy(
            windows.at[step, k, q],
            windows.at[step, k, q],
            pass_send.at[step, k, q % half, other],
            win_recv.at[step, k, q],
            depth=other,
        )

    def sends(act):
        for q in range(slots):
            home = wrap(s - 1 - 4 * (q % quarter))

            @pl.when((home <= strips - 3) & (d == q // half))
            def _():
                for step in list(range(1, angle_devs)) + [0]:
                    for k in (0, 2, 1):
                        if not (step == 0 and own_strip(k, q)):
                            act(cut_copy(k, q, home, step))

    sends(lambda copy: copy.start())

    for q in range(slots):
        home = wrap(s - 1 - 4 * (q % quarter))
        for k in range(REACHES):
            if own_strip(k, q):

                @pl.when((home <= strips - 3) & (d == q // half))
                def _():
                    cut_local(k, q).start()

    def relays(act):
        for step in range(angle_devs):
            for k in range(REACHES):

                @pl.when(reached(k))
                def _():
                    for q in range(slots):

                        @pl.when(d == q // half)
                        def _():
                            act(step, k, q)

    def relay(step, k, q):
        if step == 0 and own_strip(k, q):
            cut_local(k, q).wait()
        else:
            cut_copy(k, q, s - k, step).wait_recv()
        for other in range(depths):
            if other != q // half:
                pass_copy(step, k, q, other).start()

    relays(relay)

    for step in range(angle_devs):
        for k in range(REACHES):

            @pl.when(reached(k))
            def _():
                for q in range(slots):

                    @pl.when(d != q // half)
                    def _():
                        pass_copy(step, k, q, q // half).wait_recv()

    for step in range(1, angle_devs):
        for copy in meta_copies(step):
            copy.wait_recv()

    for other in range(depths):

        @pl.when(d != other)
        def _():
            amp_copy(other).wait_send()

    for step in range(1, angle_devs):
        for copy in meta_copies(step):
            copy.wait_send()
    for k in range(REACHES):

        @pl.when(reached(k))
        def _():
            for q in range(slots):
                if own_strip(k, q):

                    @pl.when(d != q // half)
                    def _():
                        film_copy(k, q).wait_send()
                else:
                    film_copy(k, q).wait_send()

    sends(lambda copy: copy.wait_send())

    def passed(step, k, q):
        for other in range(depths):
            if other != q // half:
                pass_copy(step, k, q, other).wait_send()

    relays(passed)


def deposit_kernel(
    sizes,
    scaling,
    windows,
    shear,
    scan_y,
    slot_angle,
    owner_slot,
    shears,
    scans_y,
    slot_angles,
    owner_slots,
    out,
    placed,
    total,
):
    strips, angle_devs, depths, layers, slots, columns = sizes
    share = WX // angle_devs
    reach = share + SHEAR
    s = lax.axis_index("strip")
    groups = [(Meta(shear, owner_slot, slots, ()), scan_y, slot_angle)]
    for step in range(1, angle_devs):
        groups.append((Meta(shears, owner_slots, slots, (step,)), scans_y, slot_angles))

    total[...] = jnp.zeros_like(total)
    for k in range(REACHES):
        home = s - k

        @pl.when((home >= 0) & (home <= strips - 3))
        def _():
            lifts = []
            for step in range(angle_devs):
                meta, corners, angles = groups[step]
                for q in range(slots):
                    at = (step * slots + q) * reach
                    window = one_hot(differences(FRAME, columns) == meta.pick(corners, home, q))
                    value = windows[step, k, q]
                    for part in range(2):
                        placed[at : at + reach, part * columns : (part + 1) * columns] = dot(
                            value[:, part * FRAME : (part + 1) * FRAME], window
                        ).astype(jnp.bfloat16)
                    angle = meta.pick(angles, home, q)
                    lifts.append([meta.shear(angle, z) for z in range(layers)])
            gap = differences(share, reach)
            for i, lift in enumerate(lifts):
                picks = jnp.concatenate(
                    [one_hot(gap == SHEAR - 1 - lift[z]) for z in range(layers)], axis=0
                )
                total[...] += dot(picks, placed[i * reach : (i + 1) * reach])

    for z in range(layers):
        for part in range(2):
            out[z, part] = (
                total[z * share : (z + 1) * share, part * columns : (part + 1) * columns] * scaling
            )


def body(sizes_of, crystal, probe, amplitude, shear, scan_x, scan_y, slot_angle, owner_slot, counts):
    strips, angle_devs, depths = sizes_of
    layers, _, _, columns = crystal.shape
    slots = owner_slot.shape[2]
    half = slots // depths
    share = WX // angle_devs
    reach = share + SHEAR
    table, table_t = dft_tables()
    bf16 = jnp.bfloat16
    scan_x, scan_y, slot_angle, owner_slot = [
        jnp.swapaxes(value, 1, 2) for value in (scan_x, scan_y, slot_angle, owner_slot)
    ]
    sizes = (strips, angle_devs, depths, layers, slots, columns)
    tables = (shear, scan_y, slot_angle, owner_slot)
    anywhere = pl.BlockSpec(memory_space=pl.ANY)
    vmem = pl.BlockSpec(memory_space=pltpu.VMEM)
    smem = pl.BlockSpec(memory_space=pltpu.SMEM)
    dma = pltpu.SemaphoreType.DMA
    scratch = [
        pltpu.VMEM((layers * WX, 2 * columns), bf16),
        pltpu.VMEM(probe.shape, bf16),
        pltpu.VMEM(table.shape, bf16),
        pltpu.VMEM(table.shape, bf16),
    ]
    scratch += [pltpu.VMEM((slots, rows, 2 * FRAME), bf16) for rows in ROWS]
    scratch += [pltpu.VMEM((depths, half, rows, 2 * FRAME), bf16) for rows in ROWS]
    scratch += [
        pltpu.VMEM((depths, half, FRAME // depths, FRAME), bf16),
        pltpu.VMEM((half, REACHES, angle_devs, reach, 2 * FRAME), bf16),
        dma((2 * layers + 3,)),
        dma((REACHES, slots)),
        dma((REACHES, depths, half)),
        dma((depths,)),
        dma((depths,)),
        dma((angle_devs, len(tables))),
        dma((angle_devs, len(tables))),
        dma((REACHES, half, angle_devs)),
        dma((angle_devs, REACHES, half, depths)),
        dma((angle_devs, REACHES, slots)),
    ]
    windows, *others = pl.pallas_call(
        functools.partial(kernel, sizes),
        out_shape=(
            jax.ShapeDtypeStruct((angle_devs, REACHES, slots, reach, 2 * FRAME), bf16),
        )
        + tuple(jax.ShapeDtypeStruct((angle_devs,) + x.shape, jnp.int32) for x in tables),
        in_specs=[anywhere] * 5 + [smem] * 6 + [anywhere] * 4,
        out_specs=(anywhere,) * 5,
        scratch_shapes=scratch,
        compiler_params=pltpu.CompilerParams(collective_id=0, has_side_effects=True),
    )(
        crystal,
        probe,
        amplitude,
        table,
        table_t,
        shear,
        scan_x,
        scan_y,
        slot_angle,
        owner_slot,
        counts,
        *tables,
    )
    scaling = 1.0 / (shear.shape[0] * angle_devs)
    return pl.pallas_call(
        functools.partial(deposit_kernel, sizes, scaling),
        out_shape=jax.ShapeDtypeStruct((layers, 2, share, columns), jnp.float32),
        in_specs=[vmem] + [smem] * 8,
        out_specs=vmem,
        scratch_shapes=[
            pltpu.VMEM((angle_devs * slots * reach, 2 * columns), bf16),
            pltpu.VMEM((layers * share, 2 * columns), jnp.float32),
        ],
    )(windows, *tables, *others)


def solution(mesh):
    placed = (
        P(("groups", "depth"), None, "strip", None),
        P(),
        P("angle", ("groups", "strip", "depth"), None),
        P(("groups", "angle"), "depth"),
        P(("groups", "angle"), None, None),
        P(("groups", "angle"), None, None),
        P(("groups", "angle"), None, None),
        P(("groups", "angle"), None, None),
        P(("groups", "angle"), None),
    )
    sizes_of = (mesh.shape["strip"], mesh.shape["angle"], mesh.shape["depth"])
    return jax.shard_map(
        functools.partial(body, sizes_of),
        mesh=mesh,
        in_specs=placed,
        out_specs=P(("groups", "depth"), None, ("strip", "angle"), None),
        check_vma=False,
    )
```

```python
import functools

import jax
import jax.numpy as jnp
import numpy as np
from jax import lax
from jax.experimental import pallas as pl
from jax.experimental.pallas import tpu as pltpu
from jax.sharding import PartitionSpec as P

FRAME = 256
WX = 128
SHEAR = 16
REACHES = 3
ROWS = (WX, FRAME, FRAME - WX)
BASES = (0, 0, WX)
MESH = pl.DeviceIdType.MESH


def dft_tables():
    index_row = np.arange(FRAME)
    phase = (index_row[:, None] * index_row[None, :] % FRAME) * (2.0 * np.pi / FRAME)
    real = np.cos(phase) / np.sqrt(FRAME)
    imag = -np.sin(phase) / np.sqrt(FRAME)
    table = np.block([[real, imag], [-imag, real]]).astype(np.float32)
    return jnp.asarray(table, jnp.bfloat16), jnp.asarray(table.T, jnp.bfloat16)


def dot(left, right):
    return jnp.dot(left, right, preferred_element_type=jnp.float32)


def differences(rows, columns):
    shape = (rows, columns)
    return lax.broadcasted_iota(jnp.int32, shape, 1) - lax.broadcasted_iota(jnp.int32, shape, 0)


def one_hot(mask):
    return jnp.where(mask, 1.0, 0.0).astype(jnp.bfloat16)


class Meta:
    def __init__(self, lifts, owner_slot, slots, lead):
        self.lifts, self.owner_slot = lifts, owner_slot
        self.slots, self.lead = slots, lead

    def shear(self, angle, z):
        return self.lifts[self.lead + (angle, z)]

    def pick(self, ref, home, quota):
        value = jnp.int32(0)
        for m in range(self.slots):
            at = self.lead + (0, m, home)
            value = value + jnp.where(self.owner_slot[at] == quota, ref[at], 0)
        return value

    def slot(self, home, quota):
        value = jnp.int32(0)
        for m in range(self.slots):
            at = self.lead + (0, m, home)
            value = value + jnp.where(self.owner_slot[at] == quota, m, 0)
        return value


def kernel(
    sizes,
    crystal,
    probe_in,
    amplitude,
    table_in,
    table_t_in,
    shear,
    scan_x,
    scan_y,
    slot_angle,
    owner_slot,
    counts,
    shear_in,
    scan_y_in,
    slot_angle_in,
    owner_slot_in,
    windows,
    shear_out,
    scan_y_out,
    slot_angle_out,
    owner_slot_out,
    film,
    probe,
    table,
    table_t,
    sent0,
    sent1,
    sent2,
    got0,
    got1,
    got2,
    mix0,
    mix1,
    mix2,
    part0,
    part1,
    part2,
    own,
    measured,
    cuts,
    load_sem,
    film_send,
    film_recv,
    mix_send,
    mix_recv,
    own_send,
    own_recv,
    amp_send,
    amp_recv,
    meta_send,
    meta_recv,
    cut_send,
    pass_send,
    win_recv,
):
    strips, angle_devs, depths, layers, slots, columns = sizes
    quarter = strips // 4
    half = slots // depths
    share = WX // angle_devs
    reach = share + SHEAR
    sent = (sent0, sent1, sent2)
    got = (got0, got1, got2)
    mix = (mix0, mix1, mix2)
    parts = (part0, part1, part2)
    s = lax.axis_index("strip")
    a = lax.axis_index("angle")
    d = lax.axis_index("depth")
    meta = Meta(shear, owner_slot, slots, ())

    def rcopy(source, target, send_sem, recv_sem, **where):
        return pltpu.make_async_remote_copy(
            source, target, send_sem, recv_sem, device_id=where, device_id_type=MESH
        )

    def wrap(strip):
        return lax.rem(strip + 4 * strips, strips)

    loads = [
        pltpu.make_async_copy(
            crystal.at[layer, part],
            film.at[layer * WX : (layer + 1) * WX, part * columns : (part + 1) * columns],
            load_sem.at[layer * 2 + part],
        )
        for layer in range(layers)
        for part in range(2)
    ]
    late = [
        pltpu.make_async_copy(source, target, load_sem.at[2 * layers + i])
        for i, (source, target) in enumerate(
            ((probe_in, probe), (table_in, table), (table_t_in, table_t))
        )
    ]
    for copy in loads + late:
        copy.start()

    barrier = pltpu.get_barrier_semaphore()
    shifts = set()
    for k in range(REACHES):
        for t in range(quarter):
            shifts |= {(1 - k + 4 * t) % strips, (k - 1 - 4 * t) % strips}
    expected = jnp.int32(0)
    for shift in sorted(shifts | {0}):
        peer = wrap(s + shift)
        if quarter == 1 and shift:
            close = jnp.abs(peer - s) == 1
        else:
            close = peer >= 0
        near = angle_devs + depths - 1 - (1 if shift == 0 else 0)
        expected = expected + jnp.where(close, near, 0)

        @pl.when(close)
        def _():
            for step in range(angle_devs):
                if shift or step:
                    place = {"strip": peer, "angle": lax.rem(a + step, angle_devs)}
                    pl.semaphore_signal(barrier, 1, device_id=place, device_id_type=MESH)
            for step in range(1, depths):
                place = {"strip": peer, "depth": lax.rem(d + step, depths)}
                pl.semaphore_signal(barrier, 1, device_id=place, device_id_type=MESH)

    for copy in loads:
        copy.wait()

    def block(k, device):
        rows = ROWS[k] // depths
        return pl.ds(pl.multiple_of(device * rows, rows), rows)

    def mix_copy(k, q, step):
        target = lax.rem(d + step, depths)
        return rcopy(
            sent[k].at[q, block(k, target)],
            mix[k].at[q, step],
            mix_send.at[k, q, step],
            mix_recv.at[k, q, step],
            depth=target,
        )

    def film_copy(k, q):
        return rcopy(
            parts[k].at[q],
            got[k].at[q % half, block(k, d)],
            film_send.at[k, q],
            film_recv.at[k, d, q % half],
            strip=wrap(s - k + 4 * (q % quarter) + 1),
            depth=q // half,
        )

    def own_copy(q):
        return rcopy(
            sent[1].at[q],
            own.at[d, q % half],
            own_send.at[q],
            own_recv.at[d, q % half],
            depth=q // half,
        )

    def exchange(k, q):
        for step in range(1, depths):
            mix_copy(k, q, step).start()

    def merge(k, q):
        value = sent[k][q, block(k, d)].astype(jnp.float32)
        for step in range(1, depths):
            mix_copy(k, q, step).wait_recv()
            value = value + mix[k][q, step].astype(jnp.float32)
        parts[k][q] = value.astype(jnp.bfloat16)
        film_copy(k, q).start()

    def own_strip(k, q):
        return (1 - k + 4 * (q % quarter)) % strips == 0

    def project(k, q):
        home = s - k
        offset = meta.pick(scan_x, home, q) - WX * k + BASES[k]
        angle = meta.pick(slot_angle, home, q)
        corner = meta.pick(scan_y, home, q)
        gap = differences(ROWS[k], WX)
        picks = jnp.concatenate(
            [one_hot(gap == offset + meta.shear(angle, z)) for z in range(layers)], axis=1
        )
        tall = dot(picks, film[...]).astype(jnp.bfloat16)
        window = one_hot(differences(columns, FRAME) == -corner)
        return jnp.concatenate(
            [dot(tall[:, :columns], window), dot(tall[:, columns:], window)], axis=1
        ).astype(jnp.bfloat16)

    def reached(k):
        return (s - k >= 0) & (s - k <= strips - 3)

    for q in range(slots):
        for k in (0, 2):

            @pl.when(reached(k))
            def _():
                sent[k][q] = project(k, q)

        if q == 0:
            pl.semaphore_wait(barrier, expected)
        for k in (0, 2):

            @pl.when(reached(k))
            def _():
                exchange(k, q)

    for q in range(slots):
        for k in (0, 2):

            @pl.when(reached(k))
            def _():
                merge(k, q)

    def amp_copy(other):
        return rcopy(
            amplitude.at[other * half : (other + 1) * half],
            measured.at[d],
            amp_send.at[other],
            amp_recv.at[d],
            depth=other,
        )

    def amp_own(other):
        return pltpu.make_async_copy(
            amplitude.at[other * half : (other + 1) * half], measured.at[d], amp_recv.at[d]
        )

    tables = (
        (shear_in, shear_out),
        (scan_y_in, scan_y_out),
        (slot_angle_in, slot_angle_out),
        (owner_slot_in, owner_slot_out),
    )

    def meta_copies(step):
        return [
            rcopy(
                source,
                target.at[step],
                meta_send.at[step, i],
                meta_recv.at[step, i],
                angle=lax.rem(a + step, angle_devs),
            )
            for i, (source, target) in enumerate(tables)
        ]

    for other in range(depths):

        @pl.when(d != other)
        def _():
            amp_copy(other).start()

        @pl.when(d == other)
        def _():
            amp_own(other).start()

    for step in range(1, angle_devs):
        for copy in meta_copies(step):
            copy.start()

    @pl.when(reached(1))
    def _():
        for q in range(slots):
            sent[1][q] = project(1, q)
            if own_strip(1, q):

                @pl.when(d == q // half)
                def _():
                    own[d, q % half] = sent[1][q]

                @pl.when(d != q // half)
                def _():
                    own_copy(q).start()
            else:
                exchange(1, q)
        for q in range(slots):
            if not own_strip(1, q):
                merge(1, q)

    for copy in late:
        copy.wait()
    for other in range(depths):

        @pl.when(d != other)
        def _():
            rcopy(
                amplitude.at[other * half : (other + 1) * half],
                measured.at[other],
                amp_send.at[other],
                amp_recv.at[other],
                depth=other,
            ).wait_recv()

        @pl.when(d == other)
        def _():
            amp_own(other).wait()

    for lane in range(half):
        quota = d * half + lane
        home = wrap(s - 1 - 4 * lax.rem(quota, quarter))

        @pl.when(home <= strips - 3)
        def _():
            def arrive(k):
                for source in range(depths):
                    rows = ROWS[k] // depths
                    rcopy(
                        parts[k].at[lane],
                        got[k].at[lane, source * rows : (source + 1) * rows],
                        film_send.at[k, lane],
                        film_recv.at[k, source, lane],
                        strip=wrap(home + k),
                        depth=source,
                    ).wait_recv()

            local = wrap(home + 1) == s

            @pl.when(local)
            def _():
                value = own[d, lane].astype(jnp.float32)
                for step in range(1, depths):
                    source = lax.rem(d + step, depths)
                    rcopy(
                        sent[1].at[lane],
                        own.at[source, lane],
                        own_send.at[lane],
                        own_recv.at[source, lane],
                        depth=source,
                    ).wait_recv()
                    value = value + own[source, lane].astype(jnp.float32)
                got[1][lane] = value.astype(jnp.bfloat16)

            @pl.when(jnp.logical_not(local))
            def _():
                arrive(1)

            arrive(0)
            arrive(2)

            def gathered(ref, low, high):
                return ref[lane, low:high].astype(jnp.float32)

            whole = jnp.concatenate(
                [
                    gathered(got1, 0, WX) + gathered(got0, 0, WX),
                    gathered(got1, WX, FRAME) + gathered(got2, 0, FRAME - WX),
                ],
                axis=0,
            )
            probe_re = probe[0].astype(jnp.float32)
            probe_im = probe[1].astype(jnp.float32)
            film_re, film_im = whole[:, :FRAME], whole[:, FRAME:]
            exit_wave = jnp.concatenate(
                [probe_re * film_re - probe_im * film_im, probe_re * film_im + probe_im * film_re],
                axis=1,
            ).astype(jnp.bfloat16)
            section = dot(exit_wave, table[...]).astype(jnp.bfloat16)
            spectrum = dot(
                table_t[...], jnp.concatenate([section[:, :FRAME], section[:, FRAME:]], axis=0)
            )
            spec_re, spec_im = spectrum[:FRAME], spectrum[FRAME:]
            magnitude = jnp.sqrt(spec_re * spec_re + spec_im * spec_im)
            levels = jnp.concatenate(
                [measured[source, lane] for source in range(depths)], axis=0
            ).astype(jnp.float32)
            live = meta.slot(home, quota) < counts[0, home]
            live = jnp.where(live, 1.0, 0.0).astype(jnp.float32)
            factor = (1.0 - levels / jnp.maximum(magnitude, 1.0)) * live
            residual = jnp.concatenate([spec_re * factor, spec_im * factor], axis=1).astype(
                jnp.bfloat16
            )
            inverse = dot(residual, table_t[...]).astype(jnp.bfloat16)
            wave = dot(
                table[...], jnp.concatenate([inverse[:, :FRAME], inverse[:, FRAME:]], axis=0)
            )
            wave_re, wave_im = wave[:FRAME], wave[FRAME:]
            back = jnp.concatenate(
                [probe_re * wave_re + probe_im * wave_im, probe_re * wave_im - probe_im * wave_re],
                axis=1,
            ).astype(jnp.bfloat16)
            offset = meta.pick(scan_x, home, quota)
            gap = differences(reach, FRAME)
            for k in (2, 0, 1):
                for part in range(angle_devs):
                    first = WX * k - offset + part * share - (SHEAR - 1)
                    cuts[lane, k, part] = dot(one_hot(gap == first), back).astype(jnp.bfloat16)

    def cut_copy(k, q, home, step):
        target = lax.rem(a + step, angle_devs)
        return rcopy(
            cuts.at[q % half, k, target],
            windows.at[step, k, q],
            cut_send.at[k, q % half, step],
            win_recv.at[step, k, q],
            strip=wrap(home + k),
            angle=target,
        )

    def cut_local(k, q):
        return pltpu.make_async_copy(
            cuts.at[q % half, k, a], windows.at[0, k, q], win_recv.at[0, k, q]
        )

    def pass_copy(step, k, q, other):
        return rcopy(
            windows.at[step, k, q],
            windows.at[step, k, q],
            pass_send.at[step, k, q % half, other],
            win_recv.at[step, k, q],
            depth=other,
        )

    def sends(act):
        for q in range(slots):
            home = wrap(s - 1 - 4 * (q % quarter))

            @pl.when((home <= strips - 3) & (d == q // half))
            def _():
                for step in list(range(1, angle_devs)) + [0]:
                    for k in (0, 2, 1):
                        if not (step == 0 and own_strip(k, q)):
                            act(cut_copy(k, q, home, step))

    sends(lambda copy: copy.start())

    for q in range(slots):
        home = wrap(s - 1 - 4 * (q % quarter))
        for k in range(REACHES):
            if own_strip(k, q):

                @pl.when((home <= strips - 3) & (d == q // half))
                def _():
                    cut_local(k, q).start()

    def relays(act):
        for step in range(angle_devs):
            for k in range(REACHES):

                @pl.when(reached(k))
                def _():
                    for q in range(slots):

                        @pl.when(d == q // half)
                        def _():
                            act(step, k, q)

    def relay(step, k, q):
        if step == 0 and own_strip(k, q):
            cut_local(k, q).wait()
        else:
            cut_copy(k, q, s - k, step).wait_recv()
        for other in range(depths):
            if other != q // half:
                pass_copy(step, k, q, other).start()

    relays(relay)

    for step in range(angle_devs):
        for k in range(REACHES):

            @pl.when(reached(k))
            def _():
                for q in range(slots):

                    @pl.when(d != q // half)
                    def _():
                        pass_copy(step, k, q, q // half).wait_recv()

    for step in range(1, angle_devs):
        for copy in meta_copies(step):
            copy.wait_recv()

    for other in range(depths):

        @pl.when(d != other)
        def _():
            amp_copy(other).wait_send()

    for step in range(1, angle_devs):
        for copy in meta_copies(step):
            copy.wait_send()
    for k in range(REACHES):

        @pl.when(reached(k))
        def _():
            for q in range(slots):
                if own_strip(k, q):

                    @pl.when(d != q // half)
                    def _():
                        own_copy(q).wait_send()
                else:
                    film_copy(k, q).wait_send()
                    for step in range(1, depths):
                        mix_copy(k, q, step).wait_send()

    sends(lambda copy: copy.wait_send())

    def passed(step, k, q):
        for other in range(depths):
            if other != q // half:
                pass_copy(step, k, q, other).wait_send()

    relays(passed)


def deposit_kernel(
    sizes,
    scaling,
    windows,
    shear,
    scan_y,
    slot_angle,
    owner_slot,
    shears,
    scans_y,
    slot_angles,
    owner_slots,
    out,
    placed,
    total,
):
    strips, angle_devs, depths, layers, slots, columns = sizes
    share = WX // angle_devs
    reach = share + SHEAR
    s = lax.axis_index("strip")
    groups = [(Meta(shear, owner_slot, slots, ()), scan_y, slot_angle)]
    for step in range(1, angle_devs):
        groups.append((Meta(shears, owner_slots, slots, (step,)), scans_y, slot_angles))

    total[...] = jnp.zeros_like(total)
    for k in range(REACHES):
        home = s - k

        @pl.when((home >= 0) & (home <= strips - 3))
        def _():
            lifts = []
            for step in range(angle_devs):
                meta, corners, angles = groups[step]
                for q in range(slots):
                    at = (step * slots + q) * reach
                    window = one_hot(differences(FRAME, columns) == meta.pick(corners, home, q))
                    value = windows[step, k, q]
                    for part in range(2):
                        placed[at : at + reach, part * columns : (part + 1) * columns] = dot(
                            value[:, part * FRAME : (part + 1) * FRAME], window
                        ).astype(jnp.bfloat16)
                    angle = meta.pick(angles, home, q)
                    lifts.append([meta.shear(angle, z) for z in range(layers)])
            gap = differences(share, reach)
            for i, lift in enumerate(lifts):
                picks = jnp.concatenate(
                    [one_hot(gap == SHEAR - 1 - lift[z]) for z in range(layers)], axis=0
                )
                total[...] += dot(picks, placed[i * reach : (i + 1) * reach])

    for z in range(layers):
        for part in range(2):
            out[z, part] = (
                total[z * share : (z + 1) * share, part * columns : (part + 1) * columns] * scaling
            )


def body(sizes_of, crystal, probe, amplitude, shear, scan_x, scan_y, slot_angle, owner_slot, counts):
    strips, angle_devs, depths = sizes_of
    layers, _, _, columns = crystal.shape
    slots = owner_slot.shape[2]
    half = slots // depths
    share = WX // angle_devs
    reach = share + SHEAR
    table, table_t = dft_tables()
    bf16 = jnp.bfloat16
    scan_x, scan_y, slot_angle, owner_slot = [
        jnp.swapaxes(value, 1, 2) for value in (scan_x, scan_y, slot_angle, owner_slot)
    ]
    sizes = (strips, angle_devs, depths, layers, slots, columns)
    tables = (shear, scan_y, slot_angle, owner_slot)
    anywhere = pl.BlockSpec(memory_space=pl.ANY)
    vmem = pl.BlockSpec(memory_space=pltpu.VMEM)
    smem = pl.BlockSpec(memory_space=pltpu.SMEM)
    dma = pltpu.SemaphoreType.DMA
    scratch = [
        pltpu.VMEM((layers * WX, 2 * columns), bf16),
        pltpu.VMEM(probe.shape, bf16),
        pltpu.VMEM(table.shape, bf16),
        pltpu.VMEM(table.shape, bf16),
    ]
    scratch += [pltpu.VMEM((slots, rows, 2 * FRAME), bf16) for rows in ROWS]
    scratch += [pltpu.VMEM((half, rows, 2 * FRAME), bf16) for rows in ROWS]
    scratch += [pltpu.VMEM((slots, depths, rows // depths, 2 * FRAME), bf16) for rows in ROWS]
    scratch += [pltpu.VMEM((slots, rows // depths, 2 * FRAME), bf16) for rows in ROWS]
    scratch += [pltpu.VMEM((depths, half, FRAME, 2 * FRAME), bf16)]
    scratch += [
        pltpu.VMEM((depths, half, FRAME // depths, FRAME), bf16),
        pltpu.VMEM((half, REACHES, angle_devs, reach, 2 * FRAME), bf16),
        dma((2 * layers + 3,)),
        dma((REACHES, slots)),
        dma((REACHES, depths, half)),
        dma((REACHES, slots, depths)),
        dma((REACHES, slots, depths)),
        dma((slots,)),
        dma((depths, half)),
        dma((depths,)),
        dma((depths,)),
        dma((angle_devs, len(tables))),
        dma((angle_devs, len(tables))),
        dma((REACHES, half, angle_devs)),
        dma((angle_devs, REACHES, half, depths)),
        dma((angle_devs, REACHES, slots)),
    ]
    windows, *others = pl.pallas_call(
        functools.partial(kernel, sizes),
        out_shape=(
            jax.ShapeDtypeStruct((angle_devs, REACHES, slots, reach, 2 * FRAME), bf16),
        )
        + tuple(jax.ShapeDtypeStruct((angle_devs,) + x.shape, jnp.int32) for x in tables),
        in_specs=[anywhere] * 5 + [smem] * 6 + [anywhere] * 4,
        out_specs=(anywhere,) * 5,
        scratch_shapes=scratch,
        compiler_params=pltpu.CompilerParams(collective_id=0, has_side_effects=True),
    )(
        crystal,
        probe,
        amplitude,
        table,
        table_t,
        shear,
        scan_x,
        scan_y,
        slot_angle,
        owner_slot,
        counts,
        *tables,
    )
    scaling = 1.0 / (shear.shape[0] * angle_devs)
    return pl.pallas_call(
        functools.partial(deposit_kernel, sizes, scaling),
        out_shape=jax.ShapeDtypeStruct((layers, 2, share, columns), jnp.float32),
        in_specs=[vmem] + [smem] * 8,
        out_specs=vmem,
        scratch_shapes=[
            pltpu.VMEM((angle_devs * slots * reach, 2 * columns), bf16),
            pltpu.VMEM((layers * share, 2 * columns), jnp.float32),
        ],
    )(windows, *tables, *others)


def solution(mesh):
    placed = (
        P(("groups", "depth"), None, "strip", None),
        P(),
        P("angle", ("groups", "strip", "depth"), None),
        P(("groups", "angle"), "depth"),
        P(("groups", "angle"), None, None),
        P(("groups", "angle"), None, None),
        P(("groups", "angle"), None, None),
        P(("groups", "angle"), None, None),
        P(("groups", "angle"), None),
    )
    sizes_of = (mesh.shape["strip"], mesh.shape["angle"], mesh.shape["depth"])
    return jax.shard_map(
        functools.partial(body, sizes_of),
        mesh=mesh,
        in_specs=placed,
        out_specs=P(("groups", "depth"), None, ("strip", "angle"), None),
        check_vma=False,
    )
```

```python
import functools

import jax
import jax.numpy as jnp
import numpy as np
from jax import lax
from jax.experimental import pallas as pl
from jax.experimental.pallas import tpu as pltpu
from jax.sharding import PartitionSpec as P

FRAME = 256
WX = 128
SHEAR = 16
REACHES = 3
ROWS = (WX, FRAME, FRAME - WX)
BASES = (0, 0, WX)
MESH = pl.DeviceIdType.MESH


def dft_tables():
    index_row = np.arange(FRAME)
    phase = (index_row[:, None] * index_row[None, :] % FRAME) * (2.0 * np.pi / FRAME)
    real = np.cos(phase) / np.sqrt(FRAME)
    imag = -np.sin(phase) / np.sqrt(FRAME)
    table = np.block([[real, imag], [-imag, real]]).astype(np.float32)
    return jnp.asarray(table, jnp.bfloat16), jnp.asarray(table.T, jnp.bfloat16)


def dot(left, right):
    return jnp.dot(left, right, preferred_element_type=jnp.float32)


def differences(rows, columns):
    shape = (rows, columns)
    return lax.broadcasted_iota(jnp.int32, shape, 1) - lax.broadcasted_iota(jnp.int32, shape, 0)


def one_hot(mask):
    return jnp.where(mask, 1.0, 0.0).astype(jnp.bfloat16)


class Meta:
    def __init__(self, lifts, owner_slot, slots, lead):
        self.lifts, self.owner_slot = lifts, owner_slot
        self.slots, self.lead = slots, lead

    def shear(self, angle, z):
        return self.lifts[self.lead + (angle, z)]

    def pick(self, ref, home, quota):
        value = jnp.int32(0)
        for m in range(self.slots):
            at = self.lead + (0, m, home)
            value = value + jnp.where(self.owner_slot[at] == quota, ref[at], 0)
        return value

    def slot(self, home, quota):
        value = jnp.int32(0)
        for m in range(self.slots):
            at = self.lead + (0, m, home)
            value = value + jnp.where(self.owner_slot[at] == quota, m, 0)
        return value


def kernel(
    sizes,
    crystal,
    probe_in,
    amplitude,
    table_in,
    table_t_in,
    shear,
    scan_x,
    scan_y,
    slot_angle,
    owner_slot,
    counts,
    shear_in,
    scan_y_in,
    slot_angle_in,
    owner_slot_in,
    windows,
    shear_out,
    scan_y_out,
    slot_angle_out,
    owner_slot_out,
    film,
    probe,
    table,
    table_t,
    sent0,
    sent1,
    sent2,
    got0,
    got1,
    got2,
    mix0,
    mix1,
    mix2,
    part0,
    part1,
    part2,
    own,
    measured,
    cuts,
    load_sem,
    film_send,
    film_recv,
    mix_send,
    mix_recv,
    own_send,
    own_recv,
    amp_send,
    amp_recv,
    meta_send,
    meta_recv,
    cut_send,
    pass_send,
    win_recv,
):
    strips, angle_devs, depths, layers, slots, columns = sizes
    quarter = strips // 4
    half = slots // depths
    share = WX // angle_devs
    reach = share + SHEAR
    sent = (sent0, sent1, sent2)
    got = (got0, got1, got2)
    mix = (mix0, mix1, mix2)
    parts = (part0, part1, part2)
    s = lax.axis_index("strip")
    a = lax.axis_index("angle")
    d = lax.axis_index("depth")
    meta = Meta(shear, owner_slot, slots, ())

    def rcopy(source, target, send_sem, recv_sem, **where):
        return pltpu.make_async_remote_copy(
            source, target, send_sem, recv_sem, device_id=where, device_id_type=MESH
        )

    def wrap(strip):
        return lax.rem(strip + 4 * strips, strips)

    loads = [
        pltpu.make_async_copy(
            crystal.at[layer, part],
            film.at[layer * WX : (layer + 1) * WX, part * columns : (part + 1) * columns],
            load_sem.at[layer * 2 + part],
        )
        for layer in range(layers)
        for part in range(2)
    ]
    late = [
        pltpu.make_async_copy(source, target, load_sem.at[2 * layers + i])
        for i, (source, target) in enumerate(
            ((probe_in, probe), (table_in, table), (table_t_in, table_t))
        )
    ]
    for copy in loads + late:
        copy.start()

    barrier = pltpu.get_barrier_semaphore()
    shifts = set()
    for k in range(REACHES):
        for t in range(quarter):
            shifts |= {(1 - k + 4 * t) % strips, (k - 1 - 4 * t) % strips}
    expected = jnp.int32(0)
    for shift in sorted(shifts | {0}):
        peer = wrap(s + shift)
        if quarter == 1 and shift:
            close = jnp.abs(peer - s) == 1
        else:
            close = peer >= 0
        near = angle_devs + depths - 1 - (1 if shift == 0 else 0)
        expected = expected + jnp.where(close, near, 0)

        @pl.when(close)
        def _():
            for step in range(angle_devs):
                if shift or step:
                    place = {"strip": peer, "angle": lax.rem(a + step, angle_devs)}
                    pl.semaphore_signal(barrier, 1, device_id=place, device_id_type=MESH)
            for step in range(1, depths):
                place = {"strip": peer, "depth": lax.rem(d + step, depths)}
                pl.semaphore_signal(barrier, 1, device_id=place, device_id_type=MESH)

    for copy in loads:
        copy.wait()

    def block(k, device):
        rows = ROWS[k] // depths
        return pl.ds(pl.multiple_of(device * rows, rows), rows)

    def mix_copy(k, q, step):
        target = lax.rem(d + step, depths)
        return rcopy(
            sent[k].at[q, block(k, target)],
            mix[k].at[q, step],
            mix_send.at[k, q, step],
            mix_recv.at[k, q, step],
            depth=target,
        )

    def film_copy(k, q):
        return rcopy(
            parts[k].at[q],
            got[k].at[q % half, block(k, d)],
            film_send.at[k, q],
            film_recv.at[k, d, q % half],
            strip=wrap(s - k + 4 * (q % quarter) + 1),
            depth=q // half,
        )

    def own_copy(q):
        return rcopy(
            sent[1].at[q],
            own.at[d, q % half],
            own_send.at[q],
            own_recv.at[d, q % half],
            depth=q // half,
        )

    def exchange(k, q):
        for step in range(1, depths):
            mix_copy(k, q, step).start()

    def merge(k, q):
        value = sent[k][q, block(k, d)].astype(jnp.float32)
        for step in range(1, depths):
            mix_copy(k, q, step).wait_recv()
            value = value + mix[k][q, step].astype(jnp.float32)
        parts[k][q] = value.astype(jnp.bfloat16)
        film_copy(k, q).start()

    def own_strip(k, q):
        return (1 - k + 4 * (q % quarter)) % strips == 0

    def project(k, q):
        home = s - k
        offset = meta.pick(scan_x, home, q) - WX * k + BASES[k]
        angle = meta.pick(slot_angle, home, q)
        corner = meta.pick(scan_y, home, q)
        gap = differences(ROWS[k], WX)
        picks = jnp.concatenate(
            [one_hot(gap == offset + meta.shear(angle, z)) for z in range(layers)], axis=1
        )
        tall = dot(picks, film[...]).astype(jnp.bfloat16)
        window = one_hot(differences(columns, FRAME) == -corner)
        return jnp.concatenate(
            [dot(tall[:, :columns], window), dot(tall[:, columns:], window)], axis=1
        ).astype(jnp.bfloat16)

    def reached(k):
        return (s - k >= 0) & (s - k <= strips - 3)

    for q in range(slots):
        for k in (0, 2):

            @pl.when(reached(k))
            def _():
                sent[k][q] = project(k, q)

        if q == 0:
            pl.semaphore_wait(barrier, expected)
        for k in (0, 2):

            @pl.when(reached(k))
            def _():
                exchange(k, q)

    for q in range(slots):
        for k in (0, 2):

            @pl.when(reached(k))
            def _():
                merge(k, q)

    def amp_copy(other):
        return rcopy(
            amplitude.at[other * half : (other + 1) * half],
            measured.at[d],
            amp_send.at[other],
            amp_recv.at[d],
            depth=other,
        )

    def amp_own(other):
        return pltpu.make_async_copy(
            amplitude.at[other * half : (other + 1) * half], measured.at[d], amp_recv.at[d]
        )

    tables = (
        (shear_in, shear_out),
        (scan_y_in, scan_y_out),
        (slot_angle_in, slot_angle_out),
        (owner_slot_in, owner_slot_out),
    )

    def meta_copies(step):
        return [
            rcopy(
                source,
                target.at[step],
                meta_send.at[step, i],
                meta_recv.at[step, i],
                angle=lax.rem(a + step, angle_devs),
            )
            for i, (source, target) in enumerate(tables)
        ]

    for other in range(depths):

        @pl.when(d != other)
        def _():
            amp_copy(other).start()

        @pl.when(d == other)
        def _():
            amp_own(other).start()

    for step in range(1, angle_devs):
        for copy in meta_copies(step):
            copy.start()

    @pl.when(reached(1))
    def _():
        for q in range(slots):
            sent[1][q] = project(1, q)
            if own_strip(1, q):

                @pl.when(d == q // half)
                def _():
                    own[d, q % half] = sent[1][q]

                @pl.when(d != q // half)
                def _():
                    own_copy(q).start()
            else:
                exchange(1, q)
        for q in range(slots):
            if not own_strip(1, q):
                merge(1, q)

    for copy in late:
        copy.wait()
    for other in range(depths):

        @pl.when(d != other)
        def _():
            rcopy(
                amplitude.at[other * half : (other + 1) * half],
                measured.at[other],
                amp_send.at[other],
                amp_recv.at[other],
                depth=other,
            ).wait_recv()

        @pl.when(d == other)
        def _():
            amp_own(other).wait()

    for lane in range(half):
        quota = d * half + lane
        home = wrap(s - 1 - 4 * lax.rem(quota, quarter))

        @pl.when(home <= strips - 3)
        def _():
            def arrive(k):
                for source in range(depths):
                    rows = ROWS[k] // depths
                    rcopy(
                        parts[k].at[lane],
                        got[k].at[lane, source * rows : (source + 1) * rows],
                        film_send.at[k, lane],
                        film_recv.at[k, source, lane],
                        strip=wrap(home + k),
                        depth=source,
                    ).wait_recv()

            local = wrap(home + 1) == s

            @pl.when(local)
            def _():
                value = own[d, lane].astype(jnp.float32)
                for step in range(1, depths):
                    source = lax.rem(d + step, depths)
                    rcopy(
                        sent[1].at[lane],
                        own.at[source, lane],
                        own_send.at[lane],
                        own_recv.at[source, lane],
                        depth=source,
                    ).wait_recv()
                    value = value + own[source, lane].astype(jnp.float32)
                got[1][lane] = value.astype(jnp.bfloat16)

            @pl.when(jnp.logical_not(local))
            def _():
                arrive(1)

            arrive(0)
            arrive(2)

            def gathered(ref, low, high):
                return ref[lane, low:high].astype(jnp.float32)

            whole = jnp.concatenate(
                [
                    gathered(got1, 0, WX) + gathered(got0, 0, WX),
                    gathered(got1, WX, FRAME) + gathered(got2, 0, FRAME - WX),
                ],
                axis=0,
            )
            probe_re = probe[0].astype(jnp.float32)
            probe_im = probe[1].astype(jnp.float32)
            film_re, film_im = whole[:, :FRAME], whole[:, FRAME:]
            exit_wave = jnp.concatenate(
                [probe_re * film_re - probe_im * film_im, probe_re * film_im + probe_im * film_re],
                axis=1,
            ).astype(jnp.bfloat16)
            section = dot(exit_wave, table[...]).astype(jnp.bfloat16)
            spectrum = dot(
                table_t[...], jnp.concatenate([section[:, :FRAME], section[:, FRAME:]], axis=0)
            )
            spec_re, spec_im = spectrum[:FRAME], spectrum[FRAME:]
            magnitude = jnp.sqrt(spec_re * spec_re + spec_im * spec_im)
            levels = jnp.concatenate(
                [measured[source, lane] for source in range(depths)], axis=0
            ).astype(jnp.float32)
            live = meta.slot(home, quota) < counts[0, home]
            live = jnp.where(live, 1.0, 0.0).astype(jnp.float32)
            factor = (1.0 - levels / jnp.maximum(magnitude, 1.0)) * live
            residual = jnp.concatenate([spec_re * factor, spec_im * factor], axis=1).astype(
                jnp.bfloat16
            )
            inverse = dot(residual, table_t[...]).astype(jnp.bfloat16)
            wave = dot(
                table[...], jnp.concatenate([inverse[:, :FRAME], inverse[:, FRAME:]], axis=0)
            )
            wave_re, wave_im = wave[:FRAME], wave[FRAME:]
            back = jnp.concatenate(
                [probe_re * wave_re + probe_im * wave_im, probe_re * wave_im - probe_im * wave_re],
                axis=1,
            ).astype(jnp.bfloat16)
            offset = meta.pick(scan_x, home, quota)
            gap = differences(reach, FRAME)
            for k in (2, 0, 1):
                for part in range(angle_devs):
                    first = WX * k - offset + part * share - (SHEAR - 1)
                    cuts[lane, k, part] = dot(one_hot(gap == first), back).astype(jnp.bfloat16)

    def cut_copy(k, q, home, step):
        target = lax.rem(a + step, angle_devs)
        return rcopy(
            cuts.at[q % half, k, target],
            windows.at[step, k, q],
            cut_send.at[k, q % half, step],
            win_recv.at[step, k, q],
            strip=wrap(home + k),
            angle=target,
        )

    def cut_local(k, q):
        return pltpu.make_async_copy(
            cuts.at[q % half, k, a], windows.at[0, k, q], win_recv.at[0, k, q]
        )

    def pass_copy(step, k, q, other):
        return rcopy(
            windows.at[step, k, q],
            windows.at[step, k, q],
            pass_send.at[step, k, q % half, other],
            win_recv.at[step, k, q],
            depth=other,
        )

    def sends(act):
        for q in range(slots):
            home = wrap(s - 1 - 4 * (q % quarter))

            @pl.when((home <= strips - 3) & (d == q // half))
            def _():
                for step in list(range(1, angle_devs)) + [0]:
                    for k in (0, 2, 1):
                        if not (step == 0 and own_strip(k, q)):
                            act(cut_copy(k, q, home, step))

    sends(lambda copy: copy.start())

    for q in range(slots):
        home = wrap(s - 1 - 4 * (q % quarter))
        for k in range(REACHES):
            if own_strip(k, q):

                @pl.when((home <= strips - 3) & (d == q // half))
                def _():
                    cut_local(k, q).start()

    def relays(act):
        for step in range(angle_devs):
            for k in range(REACHES):

                @pl.when(reached(k))
                def _():
                    for q in range(slots):

                        @pl.when(d == q // half)
                        def _():
                            act(step, k, q)

    def relay(step, k, q):
        if step == 0 and own_strip(k, q):
            cut_local(k, q).wait()
        else:
            cut_copy(k, q, s - k, step).wait_recv()
        for other in range(depths):
            if other != q // half:
                pass_copy(step, k, q, other).start()

    relays(relay)

    for step in range(angle_devs):
        for k in range(REACHES):

            @pl.when(reached(k))
            def _():
                for q in range(slots):

                    @pl.when(d != q // half)
                    def _():
                        pass_copy(step, k, q, q // half).wait_recv()

    for step in range(1, angle_devs):
        for copy in meta_copies(step):
            copy.wait_recv()

    for other in range(depths):

        @pl.when(d != other)
        def _():
            amp_copy(other).wait_send()

    for step in range(1, angle_devs):
        for copy in meta_copies(step):
            copy.wait_send()
    for k in range(REACHES):

        @pl.when(reached(k))
        def _():
            for q in range(slots):
                if own_strip(k, q):

                    @pl.when(d != q // half)
                    def _():
                        own_copy(q).wait_send()
                else:
                    film_copy(k, q).wait_send()
                    for step in range(1, depths):
                        mix_copy(k, q, step).wait_send()

    sends(lambda copy: copy.wait_send())

    def passed(step, k, q):
        for other in range(depths):
            if other != q // half:
                pass_copy(step, k, q, other).wait_send()

    relays(passed)


def deposit_kernel(
    sizes,
    scaling,
    windows,
    shear,
    scan_y,
    slot_angle,
    owner_slot,
    shears,
    scans_y,
    slot_angles,
    owner_slots,
    out,
    placed,
    total,
):
    strips, angle_devs, depths, layers, slots, columns = sizes
    share = WX // angle_devs
    reach = share + SHEAR
    stride = -(-reach // 128) * 128
    s = lax.axis_index("strip")
    first = jnp.maximum(s - strips + 3, 0)
    groups = [(Meta(shear, owner_slot, slots, ()), scan_y, slot_angle)]
    for step in range(1, angle_devs):
        groups.append((Meta(shears, owner_slots, slots, (step,)), scans_y, slot_angles))

    for i in range(angle_devs * slots):
        placed[i * stride + reach : (i + 1) * stride] = jnp.zeros(
            (stride - reach, 2 * columns), jnp.bfloat16
        )
    for k in range(REACHES):
        home = s - k

        @pl.when((home >= 0) & (home <= strips - 3))
        def _():
            lifts = []
            for step in range(angle_devs):
                meta, corners, angles = groups[step]
                for q in range(slots):
                    at = (step * slots + q) * stride
                    corner = meta.pick(corners, home, q)
                    value = windows[step, k, q].astype(jnp.float32)
                    margin = jnp.zeros((reach, columns - FRAME), jnp.float32)
                    for part in range(2):
                        wide = jnp.concatenate(
                            [value[:, part * FRAME : (part + 1) * FRAME], margin], axis=1
                        )
                        placed[at : at + reach, part * columns : (part + 1) * columns] = pltpu.roll(
                            wide, corner, 1
                        ).astype(jnp.bfloat16)
                    angle = meta.pick(angles, home, q)
                    lifts.append([meta.shear(angle, z) for z in range(layers)])
            gap = differences(share, stride)
            picks = jnp.concatenate(
                [
                    jnp.concatenate([one_hot(gap == SHEAR - 1 - lift[z]) for lift in lifts], axis=1)
                    for z in range(layers)
                ],
                axis=0,
            )

            @pl.when(first == k)
            def _():
                total[...] = dot(picks, placed[...])

            @pl.when(first != k)
            def _():
                total[...] += dot(picks, placed[...])

    for z in range(layers):
        for part in range(2):
            out[z, part] = (
                total[z * share : (z + 1) * share, part * columns : (part + 1) * columns] * scaling
            )


def body(sizes_of, crystal, probe, amplitude, shear, scan_x, scan_y, slot_angle, owner_slot, counts):
    strips, angle_devs, depths = sizes_of
    layers, _, _, columns = crystal.shape
    slots = owner_slot.shape[2]
    half = slots // depths
    share = WX // angle_devs
    reach = share + SHEAR
    stride = -(-reach // 128) * 128
    table, table_t = dft_tables()
    bf16 = jnp.bfloat16
    scan_x, scan_y, slot_angle, owner_slot = [
        jnp.swapaxes(value, 1, 2) for value in (scan_x, scan_y, slot_angle, owner_slot)
    ]
    sizes = (strips, angle_devs, depths, layers, slots, columns)
    tables = (shear, scan_y, slot_angle, owner_slot)
    anywhere = pl.BlockSpec(memory_space=pl.ANY)
    vmem = pl.BlockSpec(memory_space=pltpu.VMEM)
    smem = pl.BlockSpec(memory_space=pltpu.SMEM)
    dma = pltpu.SemaphoreType.DMA
    scratch = [
        pltpu.VMEM((layers * WX, 2 * columns), bf16),
        pltpu.VMEM(probe.shape, bf16),
        pltpu.VMEM(table.shape, bf16),
        pltpu.VMEM(table.shape, bf16),
    ]
    scratch += [pltpu.VMEM((slots, rows, 2 * FRAME), bf16) for rows in ROWS]
    scratch += [pltpu.VMEM((half, rows, 2 * FRAME), bf16) for rows in ROWS]
    scratch += [pltpu.VMEM((slots, depths, rows // depths, 2 * FRAME), bf16) for rows in ROWS]
    scratch += [pltpu.VMEM((slots, rows // depths, 2 * FRAME), bf16) for rows in ROWS]
    scratch += [pltpu.VMEM((depths, half, FRAME, 2 * FRAME), bf16)]
    scratch += [
        pltpu.VMEM((depths, half, FRAME // depths, FRAME), bf16),
        pltpu.VMEM((half, REACHES, angle_devs, reach, 2 * FRAME), bf16),
        dma((2 * layers + 3,)),
        dma((REACHES, slots)),
        dma((REACHES, depths, half)),
        dma((REACHES, slots, depths)),
        dma((REACHES, slots, depths)),
        dma((slots,)),
        dma((depths, half)),
        dma((depths,)),
        dma((depths,)),
        dma((angle_devs, len(tables))),
        dma((angle_devs, len(tables))),
        dma((REACHES, half, angle_devs)),
        dma((angle_devs, REACHES, half, depths)),
        dma((angle_devs, REACHES, slots)),
    ]
    windows, *others = pl.pallas_call(
        functools.partial(kernel, sizes),
        out_shape=(
            jax.ShapeDtypeStruct((angle_devs, REACHES, slots, reach, 2 * FRAME), bf16),
        )
        + tuple(jax.ShapeDtypeStruct((angle_devs,) + x.shape, jnp.int32) for x in tables),
        in_specs=[anywhere] * 5 + [smem] * 6 + [anywhere] * 4,
        out_specs=(anywhere,) * 5,
        scratch_shapes=scratch,
        compiler_params=pltpu.CompilerParams(collective_id=0, has_side_effects=True),
    )(
        crystal,
        probe,
        amplitude,
        table,
        table_t,
        shear,
        scan_x,
        scan_y,
        slot_angle,
        owner_slot,
        counts,
        *tables,
    )
    scaling = 1.0 / (shear.shape[0] * angle_devs)
    return pl.pallas_call(
        functools.partial(deposit_kernel, sizes, scaling),
        out_shape=jax.ShapeDtypeStruct((layers, 2, share, columns), jnp.float32),
        in_specs=[vmem] + [smem] * 8,
        out_specs=vmem,
        scratch_shapes=[
            pltpu.VMEM((angle_devs * slots * stride, 2 * columns), bf16),
            pltpu.VMEM((layers * share, 2 * columns), jnp.float32),
        ],
    )(windows, *tables, *others)


def solution(mesh):
    placed = (
        P(("groups", "depth"), None, "strip", None),
        P(),
        P("angle", ("groups", "strip", "depth"), None),
        P(("groups", "angle"), "depth"),
        P(("groups", "angle"), None, None),
        P(("groups", "angle"), None, None),
        P(("groups", "angle"), None, None),
        P(("groups", "angle"), None, None),
        P(("groups", "angle"), None),
    )
    sizes_of = (mesh.shape["strip"], mesh.shape["angle"], mesh.shape["depth"])
    return jax.shard_map(
        functools.partial(body, sizes_of),
        mesh=mesh,
        in_specs=placed,
        out_specs=P(("groups", "depth"), None, ("strip", "angle"), None),
        check_vma=False,
    )
```
